256 devices in a mesh: mic: 4 (over y), seq: 64 (over z, x, core).
Axes of the slice: x: 4, y: 4, z: 8, core: 2. Of those that a mesh axis runs over, the one named last changes fastest.
Arguments:
- frames_in: bfloat16 [8, 32768, 512], P('mic', 'seq'), may hold values from -16 to 16
- w_qkv: bfloat16 [8, 512, 1536], P('mic'), may hold values from -0.25 to 0.25
- w_join: bfloat16 [4096, 1024], P(('mic', 'seq')), may hold values from -0.09375 to 0.09375
- norm_gain: float32 [1024], replicated, may hold values from 0.5 to 2
- w_router: bfloat16 [1024, 64], replicated, may hold values from -0.1875 to 0.1875
- w_gate: bfloat16 [64, 1024, 4096], P('seq', None, 'mic'), may hold values from -0.1875 to 0.1875
- w_up: bfloat16 [64, 1024, 4096], P('seq', None, 'mic'), may hold values from -0.1875 to 0.1875
- w_down: bfloat16 [64, 4096, 1024], P('seq', 'mic'), may hold values from -0.09375 to 0.09375
- expert_ids: int32 [64, 4, 128, 2], P('seq', 'mic'), may hold values from 0 to 63, all different within a row; in each aligned block of 128 rows (0 to 127, 128 to 255, ..., all dimensions but the last counted through in order) at most 6 rows name the same one
Outputs:
- layer_out: bfloat16 [64, 4, 128, 1024], P('seq', 'mic')
The draws below stay inside these ranges and needn't reach their ends.
Inputs may be any that keep to these rules, and one draw needn't show every extreme that they name: `expert_ids`: in the rows of one block (128 frames) no expert is named more than 6 times, a bound that some block reaches; the two ids of a frame differ.
All inputs are finite; a program needn't handle non-finite values.
Results may differ from the reference program's by a relative error of at most 0.017.
Values may be sent and summed in bfloat16 or wider, within the bound.
A program may use at most 128 MiB of HBM per device.

```python
import math
import jax
import jax.numpy as jnp
import numpy as np
from jax import lax

MICS = 8
C = 512
HEADS = 8
D = 1024
FF = 4096
EXPERTS = 64
TOP = 2
TOK_DEV = 128
CAP = 6
SEQ_GROUPS = 64
MIC_GROUPS = 4
FRAMES = 32768
N_MIC = 4
N_SEQ = 64


def draw_frames_in(key, part):
    first_key = jax.random.fold_in(key, 0)
    base = jnp.clip(jax.random.normal(first_key, (MICS, FRAMES, C), jnp.float32), -6.0, 6.0)
    return base.astype(jnp.bfloat16)


def block_scale(key, shape, shards, smallest, top_value):
    def one(dim, shards_of):
        draws = jax.random.uniform(jax.random.fold_in(jax.random.fold_in(key, 6), dim), (shards_of,), jnp.float32, smallest / len(shards), top_value / len(shards))
        return jnp.repeat(jnp.exp(draws), shape[dim] // shards_of).reshape((-1,) + (1,) * (len(shape) - dim - 1))

    factor_of = one(*shards[0])
    for cut in shards[1:]:
        factor_of = factor_of * one(*cut)
    return factor_of


def routed_block(own_key, own, number, rows, number_of, top, limit, lean):
    ranking = jax.random.permutation(own_key, number_of)
    heavy_load, usual = shares(number_of, rows * top, limit, lean, True), shares(number_of, rows * top, limit, lean, False)
    places = jnp.arange(number_of)

    def named(tallies, offset_by):
        used = int((tallies > 0).sum())
        fixed = max(1, used // 4)
        passed = fixed + (places - fixed + offset_by * (used - fixed)) % max(1, number_of - fixed)
        return jnp.zeros((number_of,), jnp.int32).at[ranking[jnp.where(places < fixed, places, passed)]].set(jnp.asarray(tallies, jnp.int32))

    tallies = jnp.where(number % 4 == 0, named(heavy_load, number // 4), named(usual, number - number // 4 - 1))
    mixed = jax.random.permutation(jax.random.fold_in(own, 3), number_of)
    donor, receiver = mixed[0:number_of // 2 * 2:2], mixed[1:number_of // 2 * 2:2]
    room = jnp.minimum(tallies[donor] - 1, limit - tallies[receiver]) // 2
    room = jnp.where((donor == ranking[0]) | (receiver == ranking[0]) | (tallies[receiver] == 0), 0, jnp.maximum(room, 0))
    passed = jax.random.randint(jax.random.fold_in(own, 4), (number_of // 2,), 0, 1 << 20) % (room + 1)
    tallies = tallies.at[donor].add(-passed).at[receiver].add(passed)
    items = jnp.searchsorted(jnp.cumsum(tallies), jnp.arange(rows * top), side="right").astype(jnp.int32)
    grid = items.reshape(top, rows).T
    grid = grid[jax.random.permutation(jax.random.fold_in(own, 1), rows)]
    offset_by = jax.random.randint(jax.random.fold_in(own, 2), (rows, 1), 0, top)
    return jnp.take_along_axis(grid, (jnp.arange(top)[None, :] + offset_by) % top, axis=1)


def shares(amount, total, limit, skew, full):
    portions = [(1 << 20) // math.isqrt(standing ** skew) + 1 for standing in range(1, amount + 1)]
    largest = limit if full else min(limit, max(-(-total // amount), total * portions[0] // sum(portions)))
    least = 1 if total - largest >= amount - 1 else 0
    holding, rest = [largest] + [least] * (amount - 1), total - largest - least * (amount - 1)
    while rest > 0:
        candidates = [i for i in range(1, amount) if holding[i] < largest] or [i for i in range(1, amount) if holding[i] < limit]
        mass, remaining = sum([portions[i] for i in candidates]), rest
        for i in candidates:
            extra = min(limit - holding[i], max(1, remaining * portions[i] // mass), rest)
            holding[i] = holding[i] + extra
            rest = rest - extra
    return np.array(holding)


def noise(key, extent, scale, limit, cuts=(), held_as=jnp.bfloat16):
    values = jax.random.normal(key, extent, jnp.float32) * scale
    if len(cuts) > 0:
        values = block_scale(key, extent, cuts, -0.22, 0.18) * values
    return jnp.clip(values, min=-limit, max=limit).astype(held_as)


def setup_inputs(seed: int = 0) -> dict:
    key_list = jax.random.split(jax.random.key(seed), 10)
    frames_in = draw_frames_in(jax.random.fold_in(key_list[9], 71), 0)
    w_qkv = noise(key_list[1], (MICS, C, 3 * C), C ** -0.5, 0.25, ((0, 4),))
    w_join = noise(key_list[2], (MICS * C, D), (MICS * C) ** -0.5, 0.09375, ((0, 256),))
    norm_gain = jnp.clip(jnp.exp(jax.random.uniform(key_list[3], (D,), jnp.float32, math.log(0.5), math.log(2.0))), 0.5, 2.0)
    w_router = noise(key_list[4], (D, EXPERTS), D ** -0.5, 0.1875)
    w_gate = noise(key_list[5], (EXPERTS, D, FF), D ** -0.5, 0.1875, ((0, 64), (2, 4)))
    w_up = noise(key_list[6], (EXPERTS, D, FF), D ** -0.5, 0.1875, ((0, 64), (2, 4)))
    w_down = noise(key_list[7], (EXPERTS, FF, D), FF ** -0.5, 0.09375, ((0, 64), (1, 4)))
    expert_ids_keys = jax.random.split(jax.random.fold_in(key_list[8], 1), SEQ_GROUPS * MIC_GROUPS * TOK_DEV // TOK_DEV)
    expert_ids_turns = jax.random.permutation(jax.random.fold_in(key_list[8], 3), SEQ_GROUPS * MIC_GROUPS * TOK_DEV // TOK_DEV)
    expert_ids = jax.vmap(lambda own, number: routed_block(jax.random.fold_in(key_list[8], 2), own, number, TOK_DEV, EXPERTS, TOP, CAP, 2))(expert_ids_keys, expert_ids_turns).reshape((SEQ_GROUPS, MIC_GROUPS, TOK_DEV, TOP))
    return dict(frames_in=frames_in, w_qkv=w_qkv, w_join=w_join, norm_gain=norm_gain, w_router=w_router, w_gate=w_gate, w_up=w_up, w_down=w_down, expert_ids=expert_ids)


def attend_frames(projected):
    frame_count = projected.shape[1]
    head_dim = C // HEADS
    queries = projected[..., :C].reshape(MICS, frame_count, HEADS, head_dim).astype(jnp.float32)
    keys_all = projected[..., C:2 * C].reshape(MICS, frame_count, HEADS, head_dim).astype(jnp.float32)
    values_all = projected[..., 2 * C:].reshape(MICS, frame_count, HEADS, head_dim).astype(jnp.float32)
    scores = jnp.einsum('ifhd,jfhd->fhij', queries, keys_all) * head_dim ** (-0.5)
    row_max = lax.optimization_barrier(jnp.max(scores, axis=-1, keepdims=True))
    weights = jnp.exp(scores - row_max)
    probs = (weights / lax.optimization_barrier(jnp.sum(weights, axis=-1, keepdims=True))).astype(jnp.bfloat16)
    mixed_heads = jnp.einsum('fhij,jfhd->fihd', probs.astype(jnp.float32), values_all)
    return mixed_heads.astype(jnp.bfloat16).reshape(frame_count, MICS * C)

def route_maps(expert_rows, expert_count, capacity):
    chosen = (expert_rows[..., None] == jnp.arange(expert_count, dtype=jnp.int32)).astype(jnp.int32)
    counts = lax.optimization_barrier(jnp.sum(chosen, axis=-2))
    before = jnp.cumsum(counts, axis=-2) - counts
    slot_index = lax.optimization_barrier(jnp.sum(before[..., None, :] * chosen, axis=-1))
    in_slot = slot_index[..., None] == jnp.arange(capacity, dtype=jnp.int32)
    mapped = (chosen[..., :, None] == 1) & in_slot[..., None, :]
    return mapped.reshape(expert_rows.shape + (expert_count * capacity,)).astype(jnp.bfloat16)

def gate_pair(logits, expert_rows):
    chosen = (expert_rows[..., None] == jnp.arange(logits.shape[-1], dtype=jnp.int32)).astype(jnp.float32)
    picked = lax.optimization_barrier(jnp.sum(logits[..., None, :] * chosen, axis=-1))
    first_gate = 1.0 / (1.0 + jnp.exp(picked[..., 1] - picked[..., 0]))
    return jnp.stack([first_gate, 1.0 - first_gate], axis=-1)

def reference(frames_in, w_qkv, w_join, norm_gain, w_router, w_gate, w_up, w_down, expert_ids):
    group_span = N_MIC * TOK_DEV
    grouped = jnp.moveaxis(frames_in.reshape(MICS, N_SEQ, group_span, C), 1, 0)

    def front(pair):
        group_frames, group_ids = pair
        projected = jnp.einsum('mfc,mce->mfe', group_frames.astype(jnp.float32), w_qkv.astype(jnp.float32)).astype(jnp.bfloat16)
        attended = attend_frames(projected)
        joined = jnp.dot(attended, w_join, preferred_element_type=jnp.float32)
        scale_row = lax.rsqrt(lax.optimization_barrier(jnp.mean(joined * joined, axis=-1, keepdims=True)) + 1e-06)
        normed = (joined * scale_row * norm_gain).astype(jnp.bfloat16)
        logits = jnp.dot(normed, w_router, preferred_element_type=jnp.float32)
        gates = gate_pair(logits.reshape(N_MIC, TOK_DEV, EXPERTS), group_ids)
        mapped = route_maps(group_ids, EXPERTS, CAP)
        merged_map = lax.optimization_barrier(jnp.sum(mapped.astype(jnp.float32), axis=2))
        buffers = jnp.einsum('prs,prd->psd', merged_map, normed.reshape(N_MIC, TOK_DEV, D).astype(jnp.float32)).astype(jnp.bfloat16)
        return (joined.reshape(N_MIC, TOK_DEV, D), gates, buffers)
    joined_all, gates_all, buffers_all = lax.map(front, (grouped, expert_ids))
    by_expert = jnp.moveaxis(buffers_all.reshape(N_SEQ, N_MIC, EXPERTS, CAP, D), 2, 0)
    part_width = FF // N_MIC

    def expert_apply(pack):
        slots, gate_w, up_w, down_w = pack
        flat = slots.reshape(-1, D)
        running = jnp.zeros((flat.shape[0], D), jnp.float32)
        for index_part in range(N_MIC):
            low = index_part * part_width
            high = low + part_width
            first_proj = jnp.dot(flat, gate_w[:, low:high], preferred_element_type=jnp.float32)
            second_proj = jnp.dot(flat, up_w[:, low:high], preferred_element_type=jnp.float32)
            inner = (jax.nn.silu(first_proj) * second_proj).astype(jnp.bfloat16)
            partial_out = jnp.dot(inner, down_w[low:high], preferred_element_type=jnp.float32)
            running = running + lax.optimization_barrier(partial_out.astype(jnp.bfloat16)).astype(jnp.float32)
        return running.astype(jnp.bfloat16).reshape(slots.shape)
    expert_out = lax.map(expert_apply, (by_expert, w_gate, w_up, w_down))
    returned = jnp.moveaxis(expert_out, 0, 2).reshape(N_SEQ, N_MIC, EXPERTS * CAP, D)
    mapped_all = route_maps(expert_ids, EXPERTS, CAP)
    picked_out = jnp.einsum('gprks,gpsd->gprkd', mapped_all.astype(jnp.float32), returned.astype(jnp.float32))
    total = joined_all + lax.optimization_barrier(jnp.sum(gates_all[..., None] * picked_out, axis=3))
    return total.astype(jnp.bfloat16)
```

```python
import jax
import jax.numpy as jnp
from jax import lax
from jax.experimental import pallas as pl
from jax.experimental.pallas import tpu as pltpu
from jax.sharding import PartitionSpec as P

MICS = 8
HEADS = 8
TOP = 2


def attend_kernel(x_ref, o_ref):
    mics = x_ref.shape[0]
    width = x_ref.shape[1] // 3
    head_dim = width // HEADS
    scale = head_dim ** (-0.5)

    def head(h, carry):
        base = pl.multiple_of(h * head_dim, head_dim)
        keys = [
            x_ref[j, pl.ds(width + base, head_dim), :].astype(jnp.float32)
            for j in range(mics)
        ]
        for i in range(mics):
            q = x_ref[i, pl.ds(base, head_dim), :].astype(jnp.float32)
            s = [jnp.sum(q * keys[j], axis=0, keepdims=True) * scale for j in range(mics)]
            m = s[0]
            for j in range(1, mics):
                m = jnp.maximum(m, s[j])
            e = [jnp.exp(s[j] - m) for j in range(mics)]
            den = e[0]
            for j in range(1, mics):
                den = den + e[j]
            acc = jnp.zeros((head_dim, x_ref.shape[2]), jnp.float32)
            for j in range(mics):
                p = (e[j] / den).astype(jnp.bfloat16).astype(jnp.float32)
                v = x_ref[j, pl.ds(2 * width + base, head_dim), :].astype(jnp.float32)
                acc = acc + p * v
            o_ref[i, pl.ds(base, head_dim), :] = acc.astype(o_ref.dtype)
        return carry

    lax.fori_loop(0, HEADS, head, 0)


def attend(x):
    mics, rows, frames = x.shape
    return pl.pallas_call(
        attend_kernel,
        out_shape=jax.ShapeDtypeStruct((mics, rows // 3, frames), jnp.bfloat16),
        in_specs=[pl.BlockSpec(memory_space=pltpu.VMEM)],
        out_specs=pl.BlockSpec(memory_space=pltpu.VMEM),
        cost_estimate=pl.CostEstimate(
            flops=4 * mics * mics * (rows // 3) * frames,
            transcendentals=mics * mics * HEADS * frames,
            bytes_accessed=x.size * 2 + mics * (rows // 3) * frames * 2,
        ),
    )(x)


def body(frames_in, w_qkv, w_join, norm_gain, w_router, w_gate, w_up, w_down, expert_ids):
    mic_count = lax.axis_size("mic")
    seq_count = lax.axis_size("seq")
    mic_local, span, chan_width = frames_in.shape
    frame_rows = span // mic_count
    model_width = w_join.shape[1]
    expert_count = w_router.shape[1]
    exp_local = w_gate.shape[0]
    capacity = max(2, 3 * TOP * frame_rows // (2 * expert_count))

    projected = jnp.einsum(
        "mfc,mce->mef", frames_in, w_qkv, preferred_element_type=jnp.float32
    ).astype(jnp.bfloat16)
    projected = projected.reshape(mic_local, 3 * chan_width, mic_count, frame_rows)
    arrived = lax.all_to_all(projected, "mic", split_axis=2, concat_axis=0, tiled=True)
    arrived = arrived.reshape(MICS, 3 * chan_width, frame_rows)
    attended_t = attend(arrived).reshape(mic_count, MICS * chan_width // mic_count, frame_rows)

    cols = lax.all_to_all(attended_t, "mic", split_axis=0, concat_axis=2, tiled=True)
    cols = cols.reshape(MICS * chan_width // mic_count, mic_count * frame_rows)
    w_rows = lax.all_gather(w_join, "seq", axis=0, tiled=True)
    partial = lax.dot_general(
        cols, w_rows, (((0,), (0,)), ((), ())), preferred_element_type=jnp.float32
    ).astype(jnp.bfloat16)
    joined = lax.psum_scatter(partial, "mic", scatter_dimension=0, tiled=True).astype(jnp.float32)

    scale_row = lax.rsqrt(jnp.mean(joined * joined, axis=-1, keepdims=True) + 1e-06)
    normed = (joined * scale_row * norm_gain).astype(jnp.bfloat16)
    logits = jnp.dot(normed, w_router, preferred_element_type=jnp.float32)
    expert_rows = expert_ids.reshape(frame_rows, TOP)
    chosen = (expert_rows[..., None] == jnp.arange(expert_count, dtype=jnp.int32)).astype(jnp.int32)
    picked = jnp.sum(logits[:, None, :] * chosen.astype(jnp.float32), axis=-1)
    first_gate = 1.0 / (1.0 + jnp.exp(picked[:, 1] - picked[:, 0]))
    gates = jnp.stack([first_gate, 1.0 - first_gate], axis=-1)
    counts = jnp.sum(chosen, axis=1)
    before = jnp.cumsum(counts, axis=0) - counts
    slot_index = jnp.sum(before[:, None, :] * chosen, axis=-1)
    in_slot = slot_index[..., None] == jnp.arange(capacity, dtype=jnp.int32)
    mapped = (
        ((chosen[..., :, None] == 1) & in_slot[..., None, :])
        .reshape(frame_rows, TOP, expert_count * capacity)
        .astype(jnp.bfloat16)
    )
    merged_map = jnp.sum(mapped, axis=1)
    buffers = jnp.einsum(
        "rs,rd->sd", merged_map, normed, preferred_element_type=jnp.float32
    ).astype(jnp.bfloat16)
    buffers = buffers.reshape(seq_count, exp_local * capacity, model_width)
    landed = lax.all_to_all(buffers, "seq", split_axis=0, concat_axis=0, tiled=True)
    arrived_rows = lax.all_gather(landed[None], "mic", axis=0, tiled=True)
    flat = arrived_rows.reshape(mic_count * seq_count * exp_local * capacity, model_width)
    first_proj = jnp.dot(flat, w_gate[0], preferred_element_type=jnp.float32)
    second_proj = jnp.dot(flat, w_up[0], preferred_element_type=jnp.float32)
    inner = (jax.nn.silu(first_proj) * second_proj).astype(jnp.bfloat16)
    result = jnp.dot(inner, w_down[0], preferred_element_type=jnp.float32).astype(jnp.bfloat16)
    summed = lax.psum_scatter(result, "mic", scatter_dimension=0, tiled=True)
    summed = summed.reshape(seq_count, exp_local * capacity, model_width)
    returned = lax.all_to_all(summed, "seq", split_axis=0, concat_axis=0, tiled=True)
    returned = returned.reshape(expert_count * capacity, model_width)
    picked_out = jnp.einsum("rks,sd->rkd", mapped, returned, preferred_element_type=jnp.float32)
    total = joined + jnp.sum(gates[..., None] * picked_out, axis=1)
    return total.astype(jnp.bfloat16).reshape(1, 1, frame_rows, model_width)


def solution(mesh):
    return jax.shard_map(
        body,
        mesh=mesh,
        in_specs=(
            P("mic", "seq", None),
            P("mic", None, None),
            P(("mic", "seq"), None),
            P(),
            P(),
            P("seq", None, "mic"),
            P("seq", None, "mic"),
            P("seq", "mic", None),
            P("seq", "mic", None, None),
        ),
        out_specs=P("seq", "mic", None, None),
        check_vma=False,
    )
```
